32 devices in a mesh: dp: 8 (over y, x, core), mp: 4 (over z).
Axes of the slice: x: 2, y: 2, z: 4, core: 2. Of those that a mesh axis runs over, the one named last changes fastest.
Arguments:
- token_ids: int32 [8, 128], P('dp'), may hold values from 0 to 250111
- target_ids: int32 [8, 128], P('dp'), may hold values from 0 to 250111
- segment_ids: int32 [8, 128], P('dp'), may hold values from 0 to 3, never falling along the last dimension, each value on 1 to 64 neighbouring positions
- target_length: int32 [8], P('dp'), may hold values from 64 to 128
- memory_length: int32 [8], P('dp'), may hold values from 64 to 256
- memory: bfloat16 [8, 256, 768], P('dp'), may hold values from -6 to 6
- embed_table: bfloat16 [250112, 768], P(('dp', 'mp')), may hold values from -6 to 6
- head_table: bfloat16 [250112, 768], P(('dp', 'mp')), may hold values from -0.4375 to 0.4375
- self_gain: float32 [768], replicated, may hold values from 0.5 to 1.5
- self_query: bfloat16 [768, 768], P(None, 'mp'), may hold values from -0.109375 to 0.109375
- self_kv: bfloat16 [768, 2, 768], P(None, None, 'mp'), may hold values from -0.109375 to 0.109375
- self_out: bfloat16 [768, 768], P(None, 'mp'), may hold values from -1.5 to 1.5
- cross_gain: float32 [768], replicated, may hold values from 0.5 to 1.5
- cross_query: bfloat16 [768, 768], P(None, 'mp'), may hold values from -0.109375 to 0.109375
- cross_kv: bfloat16 [768, 2, 768], P(None, None, 'mp'), may hold values from -0.109375 to 0.109375
- cross_out: bfloat16 [768, 768], P(None, 'mp'), may hold values from -2 to 2
- ffn_gain: float32 [768], replicated, may hold values from 0.5 to 1.5
- ffn_in: bfloat16 [768, 2, 2048], P(None, None, 'mp'), may hold values from -0.21875 to 0.21875
- ffn_out: bfloat16 [768, 2048], P(None, 'mp'), may hold values from -0.1875 to 0.1875
- final_gain: float32 [768], replicated, may hold values from 0.5 to 1.5
Outputs:
- loss: float32 [], replicated
- memory_grad: float32 [8, 256, 768], P('dp')
- embed_grad: float32 [250112, 768], P(('dp', 'mp'))
- head_grad: float32 [250112, 768], P(('dp', 'mp'))
- self_gain_grad: float32 [768], P('dp')
- self_query_grad: float32 [768, 768], P('dp', 'mp')
- self_kv_grad: float32 [768, 2, 768], P('dp', None, 'mp')
- self_out_grad: float32 [768, 768], P('dp', 'mp')
- cross_gain_grad: float32 [768], P('dp')
- cross_query_grad: float32 [768, 768], P('dp', 'mp')
- cross_kv_grad: float32 [768, 2, 768], P('dp', None, 'mp')
- cross_out_grad: float32 [768, 768], P('dp', 'mp')
- ffn_gain_grad: float32 [768], P('dp')
- ffn_in_grad: float32 [768, 2, 2048], P('dp', None, 'mp')
- ffn_out_grad: float32 [768, 2048], P('dp', 'mp')
- final_gain_grad: float32 [768], P('dp')
The draws below stay inside these ranges and needn't reach their ends.
Inputs may be any that keep to these rules, and one draw needn't show every extreme that they name: `segment_ids`: within a row the numbers never fall.
All inputs are finite; a program needn't handle non-finite values.
Results may differ from the reference program's by a relative error of at most 0.025.
The reference program's roundings to bfloat16 on the way count: a program that leaves them out, or rounds other values in their place, can miss the bound.
Values may be sent and summed in bfloat16 or wider, within the bound.
No kernel may reach another device: no remote copies, remote signals or barrier semaphores. Data moves between devices by JAX's collectives and lax.ppermute only.
A program may use at most 320 MiB of HBM per device.

```python
import math
import jax
import jax.numpy as jnp
import numpy as np
from jax import lax

D = 768
HEADS = 12
DH = 64
FF = 2048
V = 250112
SEQ = 128
MEM = 256
BATCH = 8


def place_ends(result, key, low, top_value):
    longest = result.shape.index(max(result.shape))
    spots = []
    for shift in (0, 1):
        where = [jax.random.randint(jax.random.fold_in(key, axis), (), 0, length) for axis, length in enumerate(result.shape)]
        where[longest] = (where[longest] + shift) % result.shape[longest]
        spots.append(tuple(where))
    return result.at[spots[0]].set(low).at[spots[1]].set(top_value)


def steps_of(own_key, shape, split, least, largest):
    level, own = 1.0, jax.random.fold_in(own_key, 6)
    for axis_at, blocks in split:
        steps = jnp.exp(jax.random.uniform(jax.random.fold_in(own, axis_at), (blocks,), jnp.float32, least / len(split), largest / len(split)))
        level = level * jnp.repeat(steps, shape[axis_at] // blocks).reshape([-1 if axis == axis_at else 1 for axis in range(len(shape))])
    return level


def wide_ids(own_key, extent, amount, skew):
    weights = [min(1 << octave, amount + 1 - (1 << octave)) * (1 << 20) // math.isqrt((1 << octave) ** skew) + 1 for octave in range((amount + 1).bit_length()) if 1 << octave <= amount]
    spread = 1 + sum(weights) // (1 << 30)
    listing = np.cumsum(np.array([max(1, weight // spread) for weight in weights]))
    pick = jax.random.randint(jax.random.fold_in(own_key, 1), extent, 0, int(listing[len(weights) - 1]))
    start = jnp.left_shift(1, jnp.searchsorted(jnp.asarray(listing, jnp.int32), pick, side="right").astype(jnp.int32))
    rank = start - 1 + jax.random.randint(jax.random.fold_in(own_key, 4), extent, 0, 1 << 30) % jnp.minimum(start, amount + 1 - start)
    return jax.random.permutation(jax.random.fold_in(own_key, 2), amount)[rank].astype(jnp.int32)


def split_up(amount, total, bound, slope):
    weights = [(1 << 20) // math.isqrt(rank ** slope) + 1 for rank in range(2, amount + 1)]
    rest, counts = total - bound - (amount - 1), [1] * (amount - 1)
    while rest > 0:
        movable = [i for i in range(amount - 1) if counts[i] < bound]
        pool, budget = sum([weights[i] for i in movable]), rest
        for i in movable:
            addition = min(bound - counts[i], max(1, budget * weights[i] // pool), rest)
            counts[i] = counts[i] + addition
            rest = rest - addition
    return np.array([bound] + counts)


def ragged(rng, amount, total, reach, lean):
    if amount == 2:
        one = jax.random.randint(rng, (), max(1, total - reach), min(reach, total - 1) + 1)
        return jnp.stack([one, total - one])
    tallies = jnp.asarray(split_up(amount, total, reach, lean), jnp.int32)
    twos = (amount - 1) // 2
    donor, sink = tallies[1:1 + 2 * twos:2], tallies[2:2 + 2 * twos:2]
    slack = jnp.minimum(donor - 1, reach - sink)
    moved = jax.random.randint(jax.random.fold_in(rng, 1), (twos,), 0, 1 << 20) % (slack + 1)
    tallies = tallies.at[1:1 + 2 * twos:2].set(donor - moved).at[2:2 + 2 * twos:2].set(sink + moved)
    return tallies[jax.random.permutation(jax.random.fold_in(rng, 2), amount)]


def scatter_about(key, shape, width, limit, pieces=(), held_as=jnp.bfloat16):
    result = width * jax.random.normal(key, shape, jnp.float32)
    if pieces:
        result = result * steps_of(key, shape, pieces, -0.22, 0.18)
    return jnp.clip(result, -limit, limit).astype(held_as)


def setup_inputs(seed: int = 0) -> dict:
    streams_of = jax.random.split(jax.random.key(seed), 21)
    return {
        "token_ids": place_ends(wide_ids(streams_of[0], (BATCH, SEQ), V, 2), jax.random.fold_in(streams_of[0], 3), 0, V - 1).astype(jnp.int32),
        "target_ids": place_ends(wide_ids(streams_of[1], (BATCH, SEQ), V, 2), jax.random.fold_in(streams_of[1], 3), 0, V - 1).astype(jnp.int32),
        "segment_ids": jax.vmap(lambda own: jnp.searchsorted(jnp.cumsum(ragged(own, 4, SEQ, SEQ // 2, 1)), jnp.arange(SEQ), side="right"))(jax.random.split(streams_of[2], BATCH)).reshape((BATCH, SEQ)).astype(jnp.int32),
        "target_length": place_ends(jax.random.randint(streams_of[3], (BATCH,), SEQ // 2, SEQ + 1), jax.random.fold_in(streams_of[3], 1), SEQ // 2, SEQ).astype(jnp.int32),
        "memory_length": place_ends(jax.random.randint(streams_of[4], (BATCH,), MEM // 4, MEM + 1), jax.random.fold_in(streams_of[4], 1), MEM // 4, MEM).astype(jnp.int32),
        "memory": scatter_about(streams_of[5], (BATCH, MEM, D), 1.0, 6.0, ((0, 8),)),
        "embed_table": scatter_about(streams_of[6], (V, D), 1.0, 6.0, ((0, 32),)),
        "head_table": scatter_about(streams_of[7], (V, D), (D // 4) ** -0.5, 0.4375, ((0, 32),)),
        "self_gain": jnp.clip(1.0 + 0.1 * jax.random.normal(streams_of[8], (D,), jnp.float32), 0.5, 1.5),
        "self_query": scatter_about(streams_of[9], (D, HEADS * DH), (4 * D) ** -0.5, 0.109375, ((1, 4),)),
        "self_kv": scatter_about(streams_of[10], (D, 2, HEADS * DH), (4 * D) ** -0.5, 0.109375, ((2, 4),)),
        "self_out": scatter_about(streams_of[11], (D, HEADS * DH), 16 ** -0.5, 1.5, ((1, 4),)),
        "cross_gain": jnp.clip(1.0 + 0.1 * jax.random.normal(streams_of[12], (D,), jnp.float32), 0.5, 1.5),
        "cross_query": scatter_about(streams_of[13], (D, HEADS * DH), (4 * D) ** -0.5, 0.109375, ((1, 4),)),
        "cross_kv": scatter_about(streams_of[14], (D, 2, HEADS * DH), (4 * D) ** -0.5, 0.109375, ((2, 4),)),
        "cross_out": scatter_about(streams_of[15], (D, HEADS * DH), 8 ** -0.5, 2.0, ((1, 4),)),
        "ffn_gain": jnp.clip(1.0 + 0.1 * jax.random.normal(streams_of[16], (D,), jnp.float32), 0.5, 1.5),
        "ffn_in": scatter_about(streams_of[17], (D, 2, FF), D ** -0.5, 0.21875, ((2, 4),)),
        "ffn_out": scatter_about(streams_of[18], (D, FF), (FF // 2) ** -0.5, 0.1875, ((1, 4),)),
        "final_gain": jnp.clip(1.0 + 0.1 * jax.random.normal(streams_of[19], (D,), jnp.float32), 0.5, 1.5),
    }


@jax.custom_vjp
def low(v):
    return lax.optimization_barrier(v.astype(jnp.bfloat16)).astype(jnp.float32)

@jax.custom_vjp
def low_back(v):
    return v

def low_keep(v):
    return (low(v), None)

def low_pass(kept, grad):
    return (grad,)

def back_keep(v):
    return (v, None)

def back_low(kept, grad):
    return (low(grad),)
low.defvjp(low_keep, low_pass)
low_back.defvjp(back_keep, back_low)
EPSILON = 1e-06
NEGATIVE = -1e+30
HIGHEST = lax.Precision.HIGHEST

def round_both(values):
    return low(low_back(values))

def rms_norm(values, gain):
    return values * lax.rsqrt(lax.optimization_barrier(jnp.mean(values * values, axis=-1, keepdims=True)) + EPSILON) * gain

def split_heads(values):
    return values.reshape(values.shape[0], values.shape[1], HEADS, DH)

def gelu_tanh(values):
    return jax.nn.gelu(values, approximate=True)

def attend(queries, key_rows, value_rows, allowed):
    scores = low_back(jnp.einsum('bqhe,bkhe->bhqk', queries, key_rows, precision=HIGHEST))
    scores = jnp.where(allowed, scores, NEGATIVE)
    log_total = jax.nn.logsumexp(scores, axis=-1, keepdims=True)
    weights = low(jnp.exp(scores - log_total))
    return jnp.einsum('bhqk,bkhe->bqhe', weights, value_rows, precision=HIGHEST)

def forward(embed_table, head_table, memory, self_gain, self_query, self_kv, self_out, cross_gain, cross_query, cross_kv, cross_out, ffn_gain, ffn_in, ffn_out, final_gain, token_ids, target_ids, segment_ids, target_length, memory_length):
    batch_rows, length = token_ids.shape
    memory_rows = memory.shape[1]
    positions = jnp.arange(length)
    states = low_back(embed_table[token_ids])
    normed_self = low(rms_norm(states, self_gain))
    queries = round_both(jnp.einsum('bld,dh->blh', normed_self, self_query, precision=HIGHEST))
    key_value = jnp.einsum('bld,dch->cblh', normed_self, self_kv, precision=HIGHEST)
    causal = positions[:, None] >= positions[None, :]
    same_segment = segment_ids[:, :, None] == segment_ids[:, None, :]
    allowed = (causal[None] & same_segment)[:, None]
    mixed = attend(split_heads(queries), split_heads(round_both(key_value[0])), split_heads(round_both(key_value[1])), allowed)
    mixed = round_both(mixed.reshape(batch_rows, length, -1))
    after_self = states + low_back(jnp.einsum('blh,dh->bld', mixed, self_out, precision=HIGHEST))
    normed_cross = low(rms_norm(after_self, cross_gain))
    cross_queries = round_both(jnp.einsum('bld,dh->blh', normed_cross, cross_query, precision=HIGHEST))
    cross_pair = jnp.einsum('bmd,dch->cbmh', memory, cross_kv, precision=HIGHEST)
    reachable = (jnp.arange(memory_rows)[None, :] < memory_length[:, None])[:, None, None, :]
    cross_mix = attend(split_heads(cross_queries), split_heads(round_both(cross_pair[0])), split_heads(round_both(cross_pair[1])), reachable)
    cross_mix = round_both(cross_mix.reshape(batch_rows, length, -1))
    after_cross = after_self + low_back(jnp.einsum('blh,dh->bld', cross_mix, cross_out, precision=HIGHEST))
    normed_ffn = low(rms_norm(after_cross, ffn_gain))
    inner_pre = jnp.einsum('bld,dcf->cblf', normed_ffn, ffn_in, precision=HIGHEST)
    gate_pre = low_back(inner_pre[0])
    up_pre = low_back(inner_pre[1])
    hidden = low(gelu_tanh(gate_pre) * up_pre)
    after_ffn = after_cross + low_back(jnp.einsum('blf,df->bld', hidden, ffn_out, precision=HIGHEST))
    final_states = low(rms_norm(after_ffn, final_gain)).reshape(batch_rows * length, -1)
    valid_mask = (positions[None, :] < target_length[:, None]).reshape(-1).astype(final_states.dtype)
    token_count = batch_rows * length
    block_size = math.gcd(token_count, 512)
    blocks = token_count // block_size

    def block_loss(block_args):
        row_block, pick_ids, keep_mask = block_args
        logits = low_back(jnp.dot(row_block, head_table.T, precision=HIGHEST, preferred_element_type=jnp.float32))
        log_total = jax.nn.logsumexp(logits, axis=-1)
        chosen = jnp.take_along_axis(logits, pick_ids[:, None], axis=1)[:, 0]
        return jnp.sum(keep_mask * (log_total - chosen))
    block_losses = lax.map(jax.checkpoint(block_loss), (final_states.reshape(blocks, block_size, -1), target_ids.reshape(blocks, block_size), valid_mask.reshape(blocks, block_size)))
    return jnp.sum(block_losses) / token_count

def reference(token_ids, target_ids, segment_ids, target_length, memory_length, memory, embed_table, head_table, self_gain, self_query, self_kv, self_out, cross_gain, cross_query, cross_kv, cross_out, ffn_gain, ffn_in, ffn_out, final_gain):
    floats = tuple((array.astype(jnp.float32) for array in (embed_table, head_table, memory, self_gain, self_query, self_kv, self_out, cross_gain, cross_query, cross_kv, cross_out, ffn_gain, ffn_in, ffn_out, final_gain)))

    def wrapped(*values):
        return forward(*values, token_ids, target_ids, segment_ids, target_length, memory_length)
    loss_value, pull_back = jax.vjp(wrapped, *floats)
    gradients = [entry.astype(jnp.float32) for entry in pull_back(jnp.ones_like(loss_value))]
    return (loss_value.astype(jnp.float32), gradients[2], gradients[0], gradients[1], gradients[3], gradients[4], gradients[5], gradients[6], gradients[7], gradients[8], gradients[9], gradients[10], gradients[11], gradients[12], gradients[13], gradients[14])
```

```python
import jax
import jax.numpy as jnp
from jax import lax
from jax.sharding import PartitionSpec as P

DH = 64

EPSILON = 1e-06
NEGATIVE = -1e30
CONTRACT_FIRST = (((0,), (0,)), ((), ()))
CONTRACT_LAST = (((1,), (1,)), ((), ()))
BF = jnp.bfloat16
F32 = jnp.float32


def normed(values, gain):
    scale_rows = lax.rsqrt(jnp.mean(values * values, axis=-1, keepdims=True) + EPSILON)
    return values * scale_rows * gain


def norm_back(values, gain, upstream):
    scale_rows = lax.rsqrt(jnp.mean(values * values, axis=-1, keepdims=True) + EPSILON)
    weighted = upstream * gain
    inner_mean = jnp.mean(values * weighted, axis=-1, keepdims=True)
    grad_values = scale_rows * weighted - values * scale_rows * scale_rows * scale_rows * inner_mean
    return (grad_values, jnp.sum(upstream * values * scale_rows, axis=0))


def gelu_tanh(values):
    return jax.nn.gelu(values, approximate=True)


def swap(values, axis, distance):
    size = lax.axis_size(axis)
    return lax.ppermute(values, axis, [(i, i ^ distance) for i in range(size)])


def model_scatter(blocks):
    total = blocks[0].astype(F32)
    sent = blocks.astype(BF)
    for k in range(1, blocks.shape[0]):
        total = total + swap(sent[k], "mp", k).astype(F32)
    return total


def model_gather(own):
    shards = lax.axis_size("mp")
    return jnp.stack([own] + [swap(own, "mp", k) for k in range(1, shards)])


def bit_orders(size):
    bits = [1 << b for b in range(1, size.bit_length() - 1)]
    return bits, bits[::-1]


def group_gather(own):
    size = lax.axis_size("dp")
    half = own.shape[0] // 2
    orders = bit_orders(size)
    parts = []
    for order, piece in zip(orders, (own[:half], own[half:])):
        held = {0: piece}
        parts.append(held)
    for step in range(len(orders[0])):
        for order, held in zip(orders, parts):
            bit = order[step]
            keys = sorted(held)
            got = swap(jnp.stack([held[g] for g in keys]), "dp", bit)
            for place, g in enumerate(keys):
                held[g ^ bit] = got[place]
    keys = sorted(parts[0])
    here = jnp.stack([jnp.concatenate([parts[0][g], parts[1][g]]) for g in keys])
    there = swap(here, "dp", 1)
    every = dict(zip(keys, here)) | {g ^ 1: there[place] for place, g in enumerate(keys)}
    return jnp.stack([every[g] for g in range(size)])


def group_scatter(blocks, merge):
    size = blocks[0].shape[0]
    half = blocks[0].shape[1] // 2
    even, odd = list(range(0, size, 2)), list(range(1, size, 2))
    sent = [jnp.stack([b[g] for g in odd]) for b in blocks]
    kept = tuple(jnp.stack([b[g] for g in even]) for b in blocks)
    kept = merge(kept, tuple(swap(s, "dp", 1) for s in sent))
    orders = bit_orders(size)
    parts = []
    for side in range(2):
        parts.append(
            (list(even), tuple(b[:, side * half : (side + 1) * half] for b in kept))
        )
    for step in range(len(orders[0])):
        for side, order in enumerate(orders):
            bit = order[step]
            keys, held = parts[side]
            stay = [i for i, g in enumerate(keys) if not g & bit]
            go = [keys.index(keys[i] ^ bit) for i in stay]
            sent = tuple(jnp.stack([b[i] for i in go]) for b in held)
            mine = tuple(jnp.stack([b[i] for i in stay]) for b in held)
            parts[side] = (
                [keys[i] for i in stay],
                merge(mine, tuple(swap(s, "dp", bit) for s in sent)),
            )
    return tuple(
        jnp.concatenate([a[0], b[0]]) for a, b in zip(parts[0][1], parts[1][1])
    )


def add_merge(mine, other):
    return tuple(a + b for a, b in zip(mine, other))


def soft_merge(mine, other):
    (values_a, total_a), (values_b, total_b) = mine, other
    total = jnp.logaddexp(total_a, total_b)
    values = values_a.astype(F32) * jnp.exp(total_a - total)[..., None] + values_b.astype(
        F32
    ) * jnp.exp(total_b - total)[..., None]
    return (values.astype(BF), total)


def rows_scatter(values):
    size, index = lax.axis_size("dp"), lax.axis_index("dp")
    rows, columns = values.shape
    values = values.astype(BF).reshape(size // 2, 2, rows // size, columns)
    mine = lax.dynamic_index_in_dim(values, index & 1, 1, keepdims=False)
    sent = lax.dynamic_index_in_dim(values, 1 - (index & 1), 1, keepdims=False)
    mine = (mine.astype(F32) + swap(sent, "dp", 1).astype(F32)).astype(BF)
    orders = bit_orders(size)
    half = columns // 2
    parts = [mine[..., :half], mine[..., half:]]
    left = [list(orders[0]), list(orders[0])]
    for step in range(len(orders[0])):
        for side, order in enumerate(orders):
            bit = order[step]
            held = parts[side]
            low = 1
            for other in left[side]:
                if other < bit:
                    low *= 2
            left[side].remove(bit)
            held = held.reshape((held.shape[0] // (2 * low), 2, low) + held.shape[1:])
            own_bit = (index // bit) & 1
            keep = lax.dynamic_index_in_dim(held, own_bit, 1, keepdims=False)
            sent = lax.dynamic_index_in_dim(held, 1 - own_bit, 1, keepdims=False)
            total = keep.astype(F32) + swap(sent, "dp", bit).astype(F32)
            total = total.reshape((total.shape[0] * low,) + total.shape[2:])
            parts[side] = total if step == len(orders[0]) - 1 else total.astype(BF)
    return jnp.concatenate([parts[0][0], parts[1][0]], axis=-1).astype(F32)


def attend(queries, key_rows, value_rows, allowed):
    scores = jnp.einsum("qhe,khe->hqk", queries, key_rows, preferred_element_type=F32)
    scores = jnp.where(allowed, scores, NEGATIVE)
    top_score = jnp.max(scores, axis=-1, keepdims=True)
    log_total = top_score + jnp.log(jnp.sum(jnp.exp(scores - top_score), axis=-1, keepdims=True))
    weights = jnp.exp(scores - log_total).astype(BF)
    mixed = jnp.einsum("hqk,khe->qhe", weights, value_rows, preferred_element_type=F32)
    return (mixed.astype(BF), log_total)


def attend_back(queries, key_rows, value_rows, allowed, log_total, upstream):
    scores = jnp.einsum("qhe,khe->hqk", queries, key_rows, preferred_element_type=F32)
    scores = jnp.where(allowed, scores, NEGATIVE)
    probs = jnp.exp(scores - log_total)
    weights = probs.astype(BF)
    pulled = jnp.einsum("qhe,khe->hqk", upstream, value_rows, preferred_element_type=F32)
    grad_scores = (probs * (pulled - jnp.sum(probs * pulled, axis=-1, keepdims=True))).astype(BF)
    grad_queries = jnp.einsum(
        "hqk,khe->qhe", grad_scores, key_rows, preferred_element_type=F32
    ).astype(BF)
    grad_keys = jnp.einsum(
        "hqk,qhe->khe", grad_scores, queries, preferred_element_type=F32
    ).astype(BF)
    grad_values = jnp.einsum(
        "hqk,qhe->khe", weights, upstream, preferred_element_type=F32
    ).astype(BF)
    return (grad_queries, grad_keys, grad_values)


def on_device(
    token_ids,
    target_ids,
    segment_ids,
    target_length,
    memory_length,
    memory,
    embed_table,
    head_table,
    self_gain,
    self_query,
    self_kv,
    self_out,
    cross_gain,
    cross_query,
    cross_kv,
    cross_out,
    ffn_gain,
    ffn_in,
    ffn_out,
    final_gain,
):
    groups = lax.axis_size("dp")
    shards = lax.axis_size("mp")
    group_index = lax.axis_index("dp")
    shard_index = lax.axis_index("mp")
    length = token_ids.shape[1]
    part_rows = length // shards
    own_rows, width = embed_table.shape
    memory_rows = memory.shape[1]
    heads_here = self_query.shape[1] // DH
    tokens = groups * length
    loss_scale = 1.0 / tokens
    own_start = (group_index * shards + shard_index) * own_rows

    shard_order = shard_index ^ jnp.arange(shards)
    group_order = group_index ^ jnp.arange(groups)

    def relative(row):
        return row.reshape(shards, part_rows)[shard_order].reshape(length)

    positions = relative(jnp.arange(length))
    segments = relative(segment_ids[0])
    marked = jnp.where(positions < target_length[0], relative(target_ids[0]), -1)
    ids_here = relative(token_ids[0])
    both = lax.all_gather(jnp.stack([ids_here, marked]), "dp", axis=0)[group_order]
    ids_every = both[:, 0].reshape(tokens)
    marked_every = both[:, 1].reshape(tokens)

    def look_up(table, ids):
        local = ids - own_start
        inside = (local >= 0) & (local < own_rows)
        rows = jnp.take(table, jnp.clip(local, 0, own_rows - 1), axis=0)
        rows = jnp.where(inside[:, None], rows, jnp.zeros((), BF))
        (mine,) = group_scatter((rows.reshape(groups, length, width),), add_merge)
        return model_scatter(mine.reshape(shards, part_rows, width))

    def spread(own):
        return model_gather(own.astype(BF)).reshape(length, width)

    def gather_sum(partial):
        return model_scatter(partial.reshape(shards, part_rows, width))

    states = look_up(embed_table, ids_every)
    normed_self = spread(normed(states, self_gain))
    queries = (
        jnp.dot(normed_self, self_query, preferred_element_type=F32)
        .astype(BF)
        .reshape(length, heads_here, DH)
    )
    key_value = (
        jnp.einsum("td,dch->cth", normed_self, self_kv, preferred_element_type=F32)
        .astype(BF)
        .reshape(2, length, heads_here, DH)
    )
    allowed = (positions[:, None] >= positions[None, :]) & (segments[:, None] == segments[None, :])
    self_mix, self_total = attend(queries, key_value[0], key_value[1], allowed)
    self_mix = self_mix.reshape(length, -1)
    after_self = states + gather_sum(
        lax.dot_general(self_mix, self_out, CONTRACT_LAST, preferred_element_type=F32)
    )
    encoder = memory[0]
    normed_cross = spread(normed(after_self, cross_gain))
    cross_queries = (
        jnp.dot(normed_cross, cross_query, preferred_element_type=F32)
        .astype(BF)
        .reshape(length, heads_here, DH)
    )
    cross_pair = (
        jnp.einsum("md,dch->cmh", encoder, cross_kv, preferred_element_type=F32)
        .astype(BF)
        .reshape(2, memory_rows, heads_here, DH)
    )
    reachable = (jnp.arange(memory_rows) < memory_length[0])[None, :]
    cross_mix, cross_total = attend(cross_queries, cross_pair[0], cross_pair[1], reachable)
    cross_mix = cross_mix.reshape(length, -1)
    after_cross = after_self + gather_sum(
        lax.dot_general(cross_mix, cross_out, CONTRACT_LAST, preferred_element_type=F32)
    )
    normed_ffn = spread(normed(after_cross, ffn_gain))
    inner_pre = jnp.einsum("td,dcf->ctf", normed_ffn, ffn_in, preferred_element_type=F32)
    up_pre = inner_pre[1]
    activated, gelu_pull = jax.vjp(gelu_tanh, inner_pre[0])
    hidden = (activated * up_pre).astype(BF)
    after_ffn = after_cross + gather_sum(
        lax.dot_general(hidden, ffn_out, CONTRACT_LAST, preferred_element_type=F32)
    )
    final_own = normed(after_ffn, final_gain).astype(BF)
    final_every = group_gather(spread(final_own)).reshape(tokens, width)
    target_rows = look_up(head_table, marked_every)

    logits = lax.dot_general(final_every, head_table, CONTRACT_LAST, preferred_element_type=F32)
    target_hit = jnp.arange(own_rows)[None, :] == (marked_every - own_start)[:, None]
    peak = jnp.max(logits, axis=1)
    raised = jnp.exp(logits - peak[:, None])
    share = jnp.sum(raised, axis=1)
    probs = jnp.where(target_hit, 0.0, raised).astype(BF)
    pulled = jnp.dot(probs, head_table, preferred_element_type=F32) / share[:, None]
    pulled, totals = group_scatter(
        (
            pulled.astype(BF).reshape(groups, length, width),
            (peak + jnp.log(share)).reshape(groups, length),
        ),
        soft_merge,
    )
    pulled = pulled.reshape(shards, part_rows, width)
    totals = totals.reshape(shards, part_rows)
    parts = [(pulled[0], totals[0])] + [
        (swap(pulled[k], "mp", k), swap(totals[k], "mp", k)) for k in range(1, shards)
    ]
    log_total = jax.nn.logsumexp(jnp.stack([t for _, t in parts]), axis=0)
    grad_final = sum(v.astype(F32) * jnp.exp(t - log_total)[:, None] for v, t in parts)
    chosen = jnp.sum(final_own.astype(F32) * target_rows, axis=1)
    keep_own = (marked[:part_rows] >= 0).astype(F32) * loss_scale
    missing = jnp.exp(chosen - log_total) - 1.0
    grad_final = (grad_final + missing[:, None] * target_rows) * keep_own[:, None]

    both = jnp.stack([log_total, missing, (log_total - chosen) * keep_own], axis=1)
    both = model_gather(both).reshape(length, 3)
    both = group_gather(both).reshape(tokens, 3)
    lines = jnp.sum(both[:, 2].reshape(groups, shards, part_rows), axis=-1)
    loss_value = jnp.sum(lines[group_order][:, shard_order])
    keep_every = (marked_every >= 0).astype(F32) * loss_scale
    factor = jnp.exp(peak - both[:, 0]) * keep_every
    grad_logits = jnp.where(
        target_hit, (both[:, 1] * keep_every)[:, None], probs.astype(F32) * factor[:, None]
    ).astype(BF)
    head_grad = lax.dot_general(
        grad_logits, final_every, CONTRACT_FIRST, preferred_element_type=F32
    )

    grad_after_ffn, final_gain_grad = norm_back(after_ffn, final_gain, grad_final)
    grad_down = spread(grad_after_ffn)
    ffn_out_grad = lax.dot_general(grad_down, hidden, CONTRACT_FIRST, preferred_element_type=F32)
    grad_hidden = jnp.dot(grad_down, ffn_out, preferred_element_type=F32)
    grad_gate = gelu_pull(grad_hidden * up_pre)[0]
    grad_inner = jnp.stack([grad_gate, grad_hidden * activated]).astype(BF)
    ffn_in_grad = jnp.einsum("td,ctf->dcf", normed_ffn, grad_inner, preferred_element_type=F32)
    grad_normed_ffn = gather_sum(
        jnp.einsum("ctf,dcf->td", grad_inner, ffn_in, preferred_element_type=F32)
    )
    grad_from_ffn, ffn_gain_grad = norm_back(after_cross, ffn_gain, grad_normed_ffn)
    grad_after_cross = grad_after_ffn + grad_from_ffn
    grad_cross_out = spread(grad_after_cross)
    cross_out_grad = lax.dot_general(
        grad_cross_out, cross_mix, CONTRACT_FIRST, preferred_element_type=F32
    )
    grad_cross_mix = (
        jnp.dot(grad_cross_out, cross_out, preferred_element_type=F32)
        .astype(BF)
        .reshape(length, heads_here, DH)
    )
    grad_cross_queries, grad_cross_keys, grad_cross_values = attend_back(
        cross_queries, cross_pair[0], cross_pair[1], reachable, cross_total, grad_cross_mix
    )
    grad_cross_queries = grad_cross_queries.reshape(length, -1)
    grad_cross_pair = jnp.stack(
        [grad_cross_keys.reshape(memory_rows, -1), grad_cross_values.reshape(memory_rows, -1)]
    )
    cross_query_grad = lax.dot_general(
        normed_cross, grad_cross_queries, CONTRACT_FIRST, preferred_element_type=F32
    )
    cross_kv_grad = jnp.einsum("md,cmh->dch", encoder, grad_cross_pair, preferred_element_type=F32)
    grad_normed_cross = gather_sum(
        lax.dot_general(grad_cross_queries, cross_query, CONTRACT_LAST, preferred_element_type=F32)
    )
    memory_part = model_scatter(
        jnp.einsum("cmh,dch->md", grad_cross_pair, cross_kv, preferred_element_type=F32).reshape(
            shards, memory_rows // shards, width
        )[shard_order]
    )
    memory_grad = model_gather(memory_part.astype(BF))[shard_order].reshape(memory_rows, width)
    memory_grad = memory_grad.astype(F32)
    grad_from_cross, cross_gain_grad = norm_back(after_self, cross_gain, grad_normed_cross)
    grad_after_self = grad_after_cross + grad_from_cross
    grad_self_out = spread(grad_after_self)
    self_out_grad = lax.dot_general(
        grad_self_out, self_mix, CONTRACT_FIRST, preferred_element_type=F32
    )
    grad_self_mix = (
        jnp.dot(grad_self_out, self_out, preferred_element_type=F32)
        .astype(BF)
        .reshape(length, heads_here, DH)
    )
    grad_queries, grad_keys, grad_values = attend_back(
        queries, key_value[0], key_value[1], allowed, self_total, grad_self_mix
    )
    grad_queries = grad_queries.reshape(length, -1)
    grad_pair = jnp.stack([grad_keys.reshape(length, -1), grad_values.reshape(length, -1)])
    self_query_grad = lax.dot_general(
        normed_self, grad_queries, CONTRACT_FIRST, preferred_element_type=F32
    )
    self_kv_grad = jnp.einsum("td,cth->dch", normed_self, grad_pair, preferred_element_type=F32)
    grad_normed_self = gather_sum(
        lax.dot_general(grad_queries, self_query, CONTRACT_LAST, preferred_element_type=F32)
        + jnp.einsum("cth,dch->td", grad_pair, self_kv, preferred_element_type=F32)
    )
    grad_from_self, self_gain_grad = norm_back(states, self_gain, grad_normed_self)
    grad_states = (grad_after_self + grad_from_self).astype(BF)
    grad_every = group_gather(spread(grad_states)).reshape(tokens, width)
    hits = (jnp.arange(own_rows)[:, None] == (ids_every - own_start)[None, :]).astype(BF)
    embed_grad = jnp.dot(hits, grad_every, preferred_element_type=F32)

    def weight_sums(pieces):
        flat = [p.reshape(p.shape[0], -1) for p in pieces]
        summed = rows_scatter(jnp.concatenate(flat, axis=1))
        results, at = [], 0
        for piece, line in zip(pieces, flat):
            part = summed[:, at : at + line.shape[1]]
            results.append(part.reshape((part.shape[0],) + piece.shape[1:]))
            at += line.shape[1]
        return results

    ffn_in_grad, ffn_out_grad = weight_sums([ffn_in_grad, ffn_out_grad])
    cross_query_grad, cross_kv_grad, cross_out_grad = weight_sums(
        [cross_query_grad, cross_kv_grad, cross_out_grad]
    )
    self_query_grad, self_kv_grad, self_out_grad = weight_sums(
        [self_query_grad, self_kv_grad, self_out_grad]
    )
    gains = jnp.stack([self_gain_grad, cross_gain_grad, ffn_gain_grad, final_gain_grad])
    gains = gains + sum(swap(gains, "mp", k) for k in range(1, shards))
    gains = gains.reshape(4, groups, width // groups)[:, group_order].transpose(1, 0, 2)
    gains = gains[0] + sum(swap(gains[g], "dp", g) for g in range(1, groups))
    return (
        loss_value,
        memory_grad[None],
        embed_grad,
        head_grad,
        gains[0],
        self_query_grad,
        self_kv_grad,
        self_out_grad,
        gains[1],
        cross_query_grad,
        cross_kv_grad,
        cross_out_grad,
        gains[2],
        ffn_in_grad,
        ffn_out_grad,
        gains[3],
    )


def solution(mesh):
    return jax.shard_map(
        on_device,
        mesh=mesh,
        in_specs=(
            P("dp", None),
            P("dp", None),
            P("dp", None),
            P("dp"),
            P("dp"),
            P("dp", None, None),
            P(("dp", "mp"), None),
            P(("dp", "mp"), None),
            P(),
            P(None, "mp"),
            P(None, None, "mp"),
            P(None, "mp"),
            P(),
            P(None, "mp"),
            P(None, None, "mp"),
            P(None, "mp"),
            P(),
            P(None, None, "mp"),
            P(None, "mp"),
            P(),
        ),
        out_specs=(
            P(),
            P("dp", None, None),
            P(("dp", "mp"), None),
            P(("dp", "mp"), None),
            P("dp"),
            P("dp", "mp"),
            P("dp", None, "mp"),
            P("dp", "mp"),
            P("dp"),
            P("dp", "mp"),
            P("dp", None, "mp"),
            P("dp", "mp"),
            P("dp"),
            P("dp", None, "mp"),
            P("dp", "mp"),
            P("dp"),
        ),
        check_vma=False,
    )
```
